32 devices in a mesh: weight: 4 (over y, x), context: 4 (over z), tensor: 2 (over core).
Axes of the slice: x: 2, y: 2, z: 4, core: 2. Of those that a mesh axis runs over, the one named last changes fastest.
Arguments:
- hidden: bfloat16 [8192, 1536], P(('weight', 'context')), may hold values from -6 to 6
- segment_ids: int32 [8192], P(('weight', 'context')), may hold values from 0 to 7, never falling along the last dimension, each value on 1 to 2048 neighbouring positions
- out_grad: bfloat16 [8192, 1536], P(('weight', 'context')), may hold values from -6 to 6
- in_gain: float32 [1536], replicated, may hold values from 0.5 to 1.5
- proj_gate: bfloat16 [1536, 3072], P(('weight', 'context'), 'tensor'), may hold values from -0.15625 to 0.15625
- proj_input: bfloat16 [1536, 3072], P(('weight', 'context'), 'tensor'), may hold values from -0.15625 to 0.15625
- proj_bc: bfloat16 [1536, 256], P(('weight', 'context')), may hold values from -0.15625 to 0.15625
- proj_step: bfloat16 [1536, 48], P(('weight', 'context'), 'tensor'), may hold values from -0.15625 to 0.15625
- conv_input: float32 [4, 3072], P(None, 'tensor'), may hold values from -3 to 3
- conv_bc: float32 [4, 256], replicated, may hold values from -3 to 3
- conv_bias_in: float32 [3072], P('tensor'), may hold values from -3 to 3
- conv_bias_bc: float32 [256], replicated, may hold values from -3 to 3
- step_bias: float32 [48], P('tensor'), may hold values from -5 to -1
- decay_log: float32 [48], P('tensor'), may hold values from -3 to 1.5
- skip_gain: float32 [48], P('tensor'), may hold values from 0.5 to 1.5
- out_gain: float32 [3072], P('tensor'), may hold values from 0.5 to 1.5
- proj_out: bfloat16 [3072, 1536], P('tensor', ('weight', 'context')), may hold values from -0.109375 to 0.109375
Outputs:
- output: bfloat16 [8192, 1536], P(('weight', 'context'))
- grad_hidden: float32 [8192, 1536], P(('weight', 'context'))
- grad_in_gain: float32 [1536], replicated
- grad_proj_gate: float32 [1536, 3072], P(('weight', 'context'), 'tensor')
- grad_proj_input: float32 [1536, 3072], P(('weight', 'context'), 'tensor')
- grad_proj_bc: float32 [1536, 256], P(('weight', 'context'))
- grad_proj_step: float32 [1536, 48], P(('weight', 'context'), 'tensor')
- grad_conv_input: float32 [4, 3072], P(None, 'tensor')
- grad_conv_bc: float32 [4, 256], replicated
- grad_conv_bias_in: float32 [3072], P('tensor')
- grad_conv_bias_bc: float32 [256], replicated
- grad_step_bias: float32 [48], P('tensor')
- grad_decay_log: float32 [48], P('tensor')
- grad_skip_gain: float32 [48], P('tensor')
- grad_out_gain: float32 [3072], P('tensor')
- grad_proj_out: float32 [3072, 1536], P('tensor', ('weight', 'context'))
The draws below stay inside these ranges and needn't reach their ends.
Inputs may be any that keep to these rules, and one draw needn't show every extreme that they name: `segment_ids`: ids never fall along the tokens; each document has 1 to (2048) tokens and one has exactly that many.
All inputs are finite; a program needn't handle non-finite values.
Results may differ from the reference program's by a relative error of at most 0.0098.
Values may be sent and summed in bfloat16 or wider, within the bound.
No kernel may reach another device: no remote copies, remote signals or barrier semaphores. Data moves between devices by JAX's collectives and lax.ppermute only.
A program may use at most 256 MiB of HBM per device.

```python
import math
import jax
import jax.numpy as jnp
import numpy as np
from jax import lax

D = 1536
HEADS = 48
HEAD_DIM = 64
STATE = 128
CONV = 4
STRETCH = 256
DI = 3072
TOK_DEV = 512
SEQ = 2048
TOKENS = 8192
N_WEIGHT = 4


def shard_levels(rng, shape, split, least, top_value):
    level = 1.0
    for dim, parts in split:
        draws = jax.random.uniform(jax.random.fold_in(jax.random.fold_in(rng, 6), dim), (parts,), jnp.float32, least / len(split), top_value / len(split))
        level = level * jnp.repeat(jnp.exp(draws), shape[dim] // parts).reshape((-1,) + (1,) * (len(shape) - 1 - dim))
    return level


def split_up(amount, total, bound, lean):
    weights = [(1 << 20) // math.isqrt(grade ** lean) + 1 for grade in range(2, amount + 1)]
    rest, counts = total - bound - (amount - 1), [1] * (amount - 1)
    while rest > 0:
        free = [i for i in range(amount - 1) if counts[i] < bound]
        mass, left = sum([weights[i] for i in free]), rest
        for i in free:
            extra = min(bound - counts[i], max(1, left * weights[i] // mass), rest)
            counts[i] = counts[i] + extra
            rest = rest - extra
    return np.array([bound] + counts)


def ragged(stream_key, amount, total, reach, slope):
    if amount == 2:
        one = jax.random.randint(stream_key, (), max(1, total - reach), min(reach, total - 1) + 1)
        return jnp.stack([one, total - one])
    tallies = jnp.asarray(split_up(amount, total, reach, slope), jnp.int32)
    twos = (amount - 1) // 2
    giver, receiver = tallies[1:1 + 2 * twos:2], tallies[2:2 + 2 * twos:2]
    room = jnp.minimum(giver - 1, reach - receiver)
    passed = jax.random.randint(jax.random.fold_in(stream_key, 1), (twos,), 0, 1 << 20) % (room + 1)
    tallies = tallies.at[1:1 + 2 * twos:2].set(giver - passed).at[2:2 + 2 * twos:2].set(receiver + passed)
    return tallies[jax.random.permutation(jax.random.fold_in(stream_key, 2), amount)]


def centred(stream_key, dims, deviation, most, split=(), held_as=jnp.bfloat16):
    values = jax.random.normal(stream_key, dims, jnp.float32) * deviation
    if len(split) > 0:
        values = shard_levels(stream_key, dims, split, -0.22, 0.18) * values
    return jnp.clip(values, min=-most, max=most).astype(held_as)


def setup_inputs(seed: int = 0) -> dict:
    arg_keys = jax.random.split(jax.random.key(seed), 18)
    return {
        "hidden": centred(arg_keys[0], (TOKENS, D), 1.0, 6.0, ((0, 16),)),
        "segment_ids": jnp.searchsorted(jnp.cumsum(ragged(arg_keys[1], TOKENS // (2 * TOK_DEV), TOKENS, 4 * TOK_DEV, 0)), jnp.arange(TOKENS), side="right").astype(jnp.int32),
        "out_grad": centred(arg_keys[2], (TOKENS, D), 1.0, 6.0, ((0, 16),)),
        "in_gain": jnp.clip(1.0 + 0.1 * jax.random.normal(arg_keys[3], (D,), jnp.float32), 0.5, 1.5),
        "proj_gate": centred(arg_keys[4], (D, DI), D ** -0.5, 0.15625, ((0, 16), (1, 2))),
        "proj_input": centred(arg_keys[5], (D, DI), D ** -0.5, 0.15625, ((0, 16), (1, 2))),
        "proj_bc": centred(arg_keys[6], (D, 2 * STATE), D ** -0.5, 0.15625, ((0, 16),)),
        "proj_step": centred(arg_keys[7], (D, HEADS), D ** -0.5, 0.15625, ((0, 16), (1, 2))),
        "conv_input": centred(arg_keys[8], (CONV, DI), 0.5, 3.0, ((1, 2),), jnp.float32),
        "conv_bc": centred(arg_keys[9], (CONV, 2 * STATE), 0.5, 3.0, (), jnp.float32),
        "conv_bias_in": centred(arg_keys[10], (DI,), 0.5, 3.0, ((0, 2),), jnp.float32),
        "conv_bias_bc": centred(arg_keys[11], (2 * STATE,), 0.5, 3.0, (), jnp.float32),
        "step_bias": jnp.clip(-5.0 + 4.0 * jax.random.uniform(arg_keys[12], (HEADS,), jnp.float32) ** shard_levels(arg_keys[12], (HEADS,), ((0, 2),), -0.2, 0.2), -5.0, -1.0),
        "decay_log": jnp.clip(-3.0 + 4.5 * jax.random.uniform(arg_keys[13], (HEADS,), jnp.float32) ** shard_levels(arg_keys[13], (HEADS,), ((0, 2),), -0.2, 0.2), -3.0, 1.5),
        "skip_gain": jnp.clip(0.5 + 1.0 * jax.random.uniform(arg_keys[14], (HEADS,), jnp.float32) ** shard_levels(arg_keys[14], (HEADS,), ((0, 2),), -0.2, 0.2), 0.5, 1.5),
        "out_gain": jnp.clip(1.0 + 0.1 * jax.random.normal(arg_keys[15], (DI,), jnp.float32), 0.5, 1.5),
        "proj_out": centred(arg_keys[16], (DI, D), DI ** -0.5, 0.109375, ((0, 2), (1, 16))),
    }


EPSILON = 1e-05
HIGHEST = lax.Precision.HIGHEST

def silu_slope(values):
    sigma = jax.nn.sigmoid(values)
    return sigma * (1.0 + values * (1.0 - sigma))

def conv_act(u_ext, kernel, offsets, same_seg):
    length = u_ext.shape[0] - 3
    total = offsets[None, :] + kernel[3][None, :] * u_ext[3:]
    for lagged in (1, 2, 3):
        total = total + kernel[3 - lagged][None, :] * same_seg[:, lagged - 1:lagged] * u_ext[3 - lagged:3 - lagged + length]
    return jax.nn.silu(total)

def ssd_stretches(x_heads, step_sizes, b_rows, c_rows, a_rate, fresh, state_in, stretch):
    length, heads, width = x_heads.shape
    count = length // stretch
    states = b_rows.shape[1]

    def one_block(state, pieces):
        x_blk, dt_blk, b_blk, c_blk, fresh_blk = pieces
        cum_log = jnp.cumsum(dt_blk * a_rate[None, :], axis=0)
        resets = jnp.cumsum(fresh_blk)
        row_idx = lax.broadcasted_iota(jnp.int32, (stretch, stretch), 0)
        col_idx = lax.broadcasted_iota(jnp.int32, (stretch, stretch), 1)
        linked = jnp.logical_and(row_idx >= col_idx, resets[:, None] == resets[None, :])
        spread = cum_log[:, None, :] - cum_log[None, :, :]
        decay_ts = jnp.exp(jnp.where(linked[:, :, None], spread, -jnp.inf))
        scores = jnp.dot(c_blk, b_blk.T, precision=HIGHEST)
        mixing = decay_ts * scores[:, :, None] * dt_blk[None, :, :]
        y_inner = jnp.einsum('tsh,shp->thp', mixing, x_blk, precision=HIGHEST)
        carried = jnp.where(resets == 0, 1.0, 0.0)[:, None] * jnp.exp(cum_log)
        y_state = jnp.einsum('tn,hpn->thp', c_blk, state, precision=HIGHEST) * carried[:, :, None]
        to_end = jnp.exp(jnp.where((resets == resets[-1])[:, None], cum_log[-1][None, :] - cum_log, -jnp.inf)) * dt_blk
        keep_end = jnp.where(resets[-1] == 0, 1.0, 0.0) * jnp.exp(cum_log[-1])
        added = jnp.einsum('sh,shp,sn->hpn', to_end, x_blk, b_blk, precision=HIGHEST)
        new_state = keep_end[:, None, None] * state + added
        return (new_state, y_inner + y_state)
    pieces = (x_heads.reshape(count, stretch, heads, width), step_sizes.reshape(count, stretch, heads), b_rows.reshape(count, stretch, states), c_rows.reshape(count, stretch, states), fresh.reshape(count, stretch))
    state_end, outputs = lax.scan(one_block, state_in, pieces)
    return (state_end, outputs.reshape(length, heads, width))

def reference(hidden, segment_ids, out_grad, in_gain, proj_gate, proj_input, proj_bc, proj_step, conv_input, conv_bc, conv_bias_in, conv_bias_bc, step_bias, decay_log, skip_gain, out_gain, proj_out):
    kernel = jnp.concatenate([conv_input, conv_bc], axis=1)
    offsets = jnp.concatenate([conv_bias_in, conv_bias_bc])
    a_rate = -jnp.exp(decay_log)
    inner = HEADS * HEAD_DIM

    def per_stream(totals, pieces):
        hid_rows, seg_rows, cot_rows = pieces
        hidden_f = hid_rows.astype(jnp.float32)
        inv_rms = lax.rsqrt(lax.optimization_barrier(jnp.mean(hidden_f * hidden_f, axis=1, keepdims=True)) + EPSILON)
        normed = (hidden_f * inv_rms * in_gain[None, :]).astype(jnp.bfloat16)
        gate_pre = jnp.dot(normed, proj_gate, preferred_element_type=jnp.float32).astype(jnp.bfloat16)
        input_pre = jnp.dot(normed, proj_input, preferred_element_type=jnp.float32).astype(jnp.bfloat16)
        bc_pre = jnp.dot(normed, proj_bc, preferred_element_type=jnp.float32).astype(jnp.bfloat16)
        step_raw = jnp.dot(normed, proj_step, preferred_element_type=jnp.float32)
        conv_in = jnp.concatenate([input_pre, bc_pre], axis=1).astype(jnp.float32)
        padded = jnp.concatenate([jnp.zeros((3, conv_in.shape[1]), jnp.float32), conv_in], axis=0)
        seg_pad = jnp.concatenate([jnp.full((3,), -1, jnp.int32), seg_rows.astype(jnp.int32)])
        same_seg = jnp.stack([(seg_pad[3 - lagged:3 - lagged + SEQ] == seg_rows).astype(jnp.float32) for lagged in (1, 2, 3)], axis=1)
        fresh = jnp.concatenate([jnp.ones((1,), jnp.int32), (seg_rows[1:] != seg_rows[:-1]).astype(jnp.int32)])

        def conv_apply(u_arg, kernel_arg, offset_arg):
            return conv_act(u_arg, kernel_arg, offset_arg, same_seg)
        conv_out, conv_pull = jax.vjp(conv_apply, padded, kernel, offsets)
        x_heads = conv_out[:, :inner].reshape(SEQ, HEADS, HEAD_DIM)
        b_rows = conv_out[:, inner:inner + STATE]
        c_rows = conv_out[:, inner + STATE:]
        step_sizes = jax.nn.softplus(step_raw + step_bias[None, :])
        zero_state = jnp.zeros((HEADS, HEAD_DIM, STATE), jnp.float32)

        def ssd_apply(x_arg, dt_arg, b_arg, c_arg, rate_arg):
            return ssd_stretches(x_arg, dt_arg, b_arg, c_arg, rate_arg, fresh, zero_state, STRETCH)[1]
        ssd_out, ssd_pull = jax.vjp(ssd_apply, x_heads, step_sizes, b_rows, c_rows, a_rate)
        y_heads = ssd_out + skip_gain[None, :, None] * x_heads
        y_flat = y_heads.reshape(SEQ, inner)
        gate_f = gate_pre.astype(jnp.float32)
        gated = y_flat * jax.nn.silu(gate_f)
        inv_out = lax.rsqrt(lax.optimization_barrier(jnp.mean(gated * gated, axis=1, keepdims=True)) + EPSILON)
        y_norm = (gated * inv_out * out_gain[None, :]).astype(jnp.bfloat16)
        mixed = jnp.dot(y_norm, proj_out, preferred_element_type=jnp.float32)
        result = (hidden_f + mixed).astype(jnp.bfloat16)
        cot_f = cot_rows.astype(jnp.float32)
        g_proj_out = jnp.dot(y_norm.T, cot_rows, preferred_element_type=jnp.float32)
        d_ynorm = jnp.dot(cot_rows, proj_out.T, preferred_element_type=jnp.float32)
        g_out_gain = lax.optimization_barrier(jnp.sum(d_ynorm * gated * inv_out, axis=0))
        d_scaled = d_ynorm * out_gain[None, :]
        d_gated = inv_out * d_scaled - gated * inv_out ** 3 * lax.optimization_barrier(jnp.mean(gated * d_scaled, axis=1, keepdims=True))
        d_yflat = d_gated * jax.nn.silu(gate_f)
        d_gate = (d_gated * y_flat * silu_slope(gate_f)).astype(jnp.bfloat16)
        d_yheads = d_yflat.reshape(SEQ, HEADS, HEAD_DIM)
        g_skip = lax.optimization_barrier(jnp.sum(d_yheads * x_heads, axis=(0, 2)))
        d_xheads, d_dt, d_brows, d_crows, d_rate = ssd_pull(d_yheads)
        d_xheads = d_xheads + skip_gain[None, :, None] * d_yheads
        d_conv = jnp.concatenate([d_xheads.reshape(SEQ, inner), d_brows, d_crows], axis=1)
        d_padded, g_kernel, g_offsets = conv_pull(d_conv)
        d_convin = d_padded[3:]
        d_input = d_convin[:, :inner].astype(jnp.bfloat16)
        d_bc = d_convin[:, inner:].astype(jnp.bfloat16)
        d_stepraw = d_dt * jax.nn.sigmoid(step_raw + step_bias[None, :])
        g_step_bias = lax.optimization_barrier(jnp.sum(d_stepraw, axis=0))
        d_step = d_stepraw.astype(jnp.bfloat16)
        g_decay = d_rate * a_rate
        d_normed = jnp.dot(d_gate, proj_gate.T, preferred_element_type=jnp.float32) + jnp.dot(d_input, proj_input.T, preferred_element_type=jnp.float32) + jnp.dot(d_step, proj_step.T, preferred_element_type=jnp.float32) + jnp.dot(d_bc, proj_bc.T, preferred_element_type=jnp.float32)
        g_in_gain = lax.optimization_barrier(jnp.sum(d_normed * hidden_f * inv_rms, axis=0))
        d_nscaled = d_normed * in_gain[None, :]
        d_hidden = inv_rms * d_nscaled - hidden_f * inv_rms ** 3 * lax.optimization_barrier(jnp.mean(hidden_f * d_nscaled, axis=1, keepdims=True)) + cot_f
        g_gate = jnp.dot(normed.T, d_gate, preferred_element_type=jnp.float32)
        g_input = jnp.dot(normed.T, d_input, preferred_element_type=jnp.float32)
        g_bc = jnp.dot(normed.T, d_bc, preferred_element_type=jnp.float32)
        g_step = jnp.dot(normed.T, d_step, preferred_element_type=jnp.float32)
        fresh_terms = (g_in_gain, g_gate, g_input, g_bc, g_step, g_kernel, g_offsets, g_step_bias, g_decay, g_skip, g_out_gain, g_proj_out)
        totals = tuple((old + new for old, new in zip(totals, fresh_terms)))
        return (totals, (result, d_hidden))
    start = (jnp.zeros((D,), jnp.float32), jnp.zeros((D, inner), jnp.float32), jnp.zeros((D, inner), jnp.float32), jnp.zeros((D, 2 * STATE), jnp.float32), jnp.zeros((D, HEADS), jnp.float32), jnp.zeros((4, inner + 2 * STATE), jnp.float32), jnp.zeros((inner + 2 * STATE,), jnp.float32), jnp.zeros((HEADS,), jnp.float32), jnp.zeros((HEADS,), jnp.float32), jnp.zeros((HEADS,), jnp.float32), jnp.zeros((inner,), jnp.float32), jnp.zeros((inner, D), jnp.float32))
    streams = (hidden.reshape(N_WEIGHT, SEQ, D), segment_ids.reshape(N_WEIGHT, SEQ), out_grad.reshape(N_WEIGHT, SEQ, D))
    totals, (results, d_hiddens) = lax.scan(per_stream, start, streams)
    g_in_gain, g_gate, g_input, g_bc, g_step, g_kernel, g_offsets, g_step_bias, g_decay, g_skip, g_out_gain, g_proj_out = totals
    return (results.reshape(TOKENS, D), d_hiddens.reshape(TOKENS, D), g_in_gain, g_gate, g_input, g_bc, g_step, g_kernel[:, :inner], g_kernel[:, inner:], g_offsets[:inner], g_offsets[inner:], g_step_bias, g_decay, g_skip, g_out_gain, g_proj_out)
```

```python
import functools

import jax
import jax.numpy as jnp
from jax import lax
from jax.experimental import pallas as pl
from jax.experimental.pallas import tpu as pltpu
from jax.sharding import PartitionSpec as P

EPSILON = 1e-05
CHUNK = 128
LOW = -1e30
F32, BF16 = jnp.float32, jnp.bfloat16


def mm(a, b):
    return lax.dot_general(a, b, (((1,), (0,)), ((), ())), preferred_element_type=F32)


def mm_nt(a, b):
    return lax.dot_general(a, b, (((1,), (1,)), ((), ())), preferred_element_type=F32)


def mm_tn(a, b):
    return lax.dot_general(a, b, (((0,), (0,)), ((), ())), preferred_element_type=F32)


def lane_low():
    return lax.broadcasted_iota(jnp.int32, (1, 128), 1) < 64


def expand(w, pairs):
    low = lane_low()
    tiles = [jnp.where(low, w[:, 2 * p : 2 * p + 1], w[:, 2 * p + 1 : 2 * p + 2]) for p in range(pairs)]
    return jnp.concatenate(tiles, axis=1)


def split2(v):
    hi = v.astype(BF16)
    return hi, (v - hi.astype(F32)).astype(BF16)


def split3(v, axis):
    one = v.astype(BF16)
    rest = v - one.astype(F32)
    two = rest.astype(BF16)
    three = (rest - two.astype(F32)).astype(BF16)
    return jnp.concatenate([one, two, three], axis=axis)


def headsum(v):
    width = v.shape[1]
    row = lax.broadcasted_iota(jnp.int32, (width, 8), 0) // 64
    col = lax.broadcasted_iota(jnp.int32, (width, 8), 1)
    pick = jnp.where(row == col, 1.0, 0.0).astype(BF16)
    hi, lo = split2(v)
    return mm(hi, pick) + mm(lo, pick)


def lower_ones():
    row = lax.broadcasted_iota(jnp.int32, (CHUNK, CHUNK), 0)
    col = lax.broadcasted_iota(jnp.int32, (CHUNK, CHUNK), 1)
    return jnp.where(row >= col, 1.0, 0.0).astype(BF16)


def upper_ones():
    row = lax.broadcasted_iota(jnp.int32, (CHUNK, CHUNK), 0)
    col = lax.broadcasted_iota(jnp.int32, (CHUNK, CHUNK), 1)
    return jnp.where(row <= col, 1.0, 0.0).astype(BF16)


def sum_cols(tri, v):
    out = mm(tri, split3(v, 1))
    return out[:, 0:8] + out[:, 8:16] + out[:, 16:24]


def sum_rows(v, tri):
    out = mm(split3(v, 0), tri)
    return out[0:8] + out[8:16] + out[16:24]


def sigmoid(v):
    return 1.0 / (1.0 + jnp.exp(-v))


def conv_total(ext, kern, segc, cur):
    total = kern[4:5, :] + kern[3:4, :] * cur
    for lagged in (1, 2, 3):
        total = total + kern[3 - lagged : 4 - lagged, :] * (
            segc[:, lagged : lagged + 1] * ext[pl.ds(8 - lagged, CHUNK), :]
        )
    return total


def state_kernel(
    inner, states, pos,
    u, uprev, uhalo, dt, dtt, segc, kern, hrow, hcol,
    x_o, b_o, c_o, cum_o, cumt_o, sl_o, se_o, ext, st,
):
    k = pl.program_id(1)
    pairs = inner // 128

    @pl.when(k == 0)
    def _():
        st[0:states, :] = jnp.zeros((states, inner), F32)
        st[states : states + 8, :] = jnp.ones((8, inner), F32)

    sl_o[0] = st[...]
    cur = u[...].astype(F32)
    before = jnp.where(k == 0, uhalo[...].astype(F32), uprev[...].astype(F32))
    ext[0:8, :] = before[8:16, :]
    ext[8 : 8 + CHUNK, :] = cur
    seg = segc[...]
    total = conv_total(ext, kern[...], seg, cur)
    act = total * sigmoid(total)
    xb = act[:, :inner].astype(BF16)
    bb = act[:, inner : inner + states].astype(BF16)
    cb = act[:, inner + states :].astype(BF16)
    x_o[...] = xb
    b_o[...] = bb
    c_o[...] = cb
    step = dt[...]
    cum = sum_cols(lower_ones(), step * hrow[0:1, :])
    cum_o[...] = cum
    cumt_o[...] = sum_rows(dtt[...] * hcol[:, 0:1], upper_ones())
    last = cum[CHUNK - 1 : CHUNK, :]
    to_end = jnp.where(seg[:, 5:6] > 0.5, jnp.exp(last - cum), 0.0) * step
    keep = expand(jnp.where(seg[CHUNK - 1 : CHUNK, 4:5] > 0.5, jnp.exp(last), 0.0), pairs)
    xw = (act[:, :inner] * expand(to_end, pairs)).astype(BF16)
    st[0:states, :] = keep * st[0:states, :] + mm_tn(bb, xw)
    st[states : states + 8, :] = keep * st[states : states + 8, :]
    se_o[0] = st[...]


def inner_kernel(inner, states, pos, x, b, c, dtt, segc, segr, cum, cumt, y_o):
    pairs = inner // 128
    low = lane_low()
    row = lax.broadcasted_iota(jnp.int32, (CHUNK, CHUNK), 0)
    col = lax.broadcasted_iota(jnp.int32, (CHUNK, CHUNK), 1)
    linked = jnp.logical_and(row >= col, segc[:, 0:1] == segr[0:1, :])
    scores = mm_nt(c[...], b[...])
    cums, cumst, steps = cum[...], cumt[...], dtt[...]
    for p in range(pairs):
        xp = x[:, 128 * p : 128 * p + 128].astype(F32)
        both = []
        for h in (2 * p, 2 * p + 1):
            fall = jnp.exp(jnp.where(linked, cums[:, h : h + 1] - cumst[h : h + 1, :], LOW))
            both.append((fall * scores * steps[h : h + 1, :]).astype(BF16))
        right = jnp.concatenate(
            [jnp.where(low, xp, 0.0).astype(BF16), jnp.where(low, 0.0, xp).astype(BF16)], axis=0
        )
        y_o[:, 128 * p : 128 * p + 128] = mm(jnp.concatenate(both, axis=1), right)


def gate_kernel(
    inner, states, pos,
    yi, x, c, cum, segc, sl, s_in, gate, dyn, chan,
    y_o, z_o, sums_o,
):
    pairs = inner // 128
    near = sl[0, 0:states, :] + sl[0, states : states + 1, :] * s_in[0].astype(F32)
    carried = jnp.where(segc[:, 4:5] > 0.5, jnp.exp(cum[...]), 0.0)
    y = yi[...] + expand(carried, pairs) * mm(c[...], near.astype(BF16))
    y = y + chan[1:2, :] * x[...].astype(F32)
    y_o[...] = y
    gf = gate[...].astype(F32)
    gated = y * (gf * sigmoid(gf))
    gain = gated * chan[0:1, :]
    z_o[...] = gain.astype(BF16)
    ones = jnp.ones((8, inner), BF16)
    sq = split2(gated * gated)
    cr = split2(gain * dyn[...].astype(F32))
    sums_o[0:1, :] = (mm_nt(ones, sq[0]) + mm_nt(ones, sq[1]))[0:1, :]
    sums_o[1:2, :] = (mm_nt(ones, cr[0]) + mm_nt(ones, cr[1]))[0:1, :]


def pull_kernel(
    inner, states, pos,
    y, x, c, cum, segc, sl, gate, dyn, scal, chan,
    dy_o, dg_o, yn_o, acc_o, pull_o,
):
    s, k = pl.program_id(0), pl.program_id(1)
    pairs = inner // 128

    @pl.when(jnp.logical_and(s == 0, k == 0))
    def _():
        acc_o[...] = jnp.zeros((8, inner), F32)

    @pl.when(k == 0)
    def _():
        pull_o[0] = jnp.zeros((states, inner), F32)

    inv, coef = scal[:, 0:1], scal[:, 1:2]
    gf = gate[...].astype(F32)
    sig = sigmoid(gf)
    yv = y[...]
    gated = yv * (gf * sig)
    normal = gated * inv
    dynf = dyn[...].astype(F32)
    d_gated = inv * (dynf * chan[0:1, :]) - gated * coef
    yn_o[...] = (normal * chan[0:1, :]).astype(BF16)
    dg_o[...] = (d_gated * yv * (sig * (1.0 + gf * (1.0 - sig)))).astype(BF16)
    d_y = d_gated * (gf * sig)
    dy_o[...] = d_y.astype(BF16)
    acc_o[0:1, :] += jnp.sum(dynf * normal, axis=0, keepdims=True)
    acc_o[1:2, :] += jnp.sum(d_y * x[...].astype(F32), axis=0, keepdims=True)
    carried = jnp.where(segc[:, 4:5] > 0.5, jnp.exp(cum[...]), 0.0)
    d_yc = d_y * (expand(carried, pairs) * sl[0, states : states + 1, :])
    pull_o[0] += mm_tn(c[...], d_yc.astype(BF16))


def back_kernel(
    inner, states, pos,
    u, uprev, uhalo, dt, segc, segr, cum, cumt, x, b, c, dy, sl, s_in, ds_end, kern, hrow, chan,
    du_o, duh_o, dac_o, dat_o, gk_o, ext, later, edge, ds,
):
    s, k = pl.program_id(0), pl.program_id(1)
    count = pl.num_programs(1)
    pairs = inner // 128
    low = lane_low()

    @pl.when(jnp.logical_and(s == 0, k == 0))
    def _():
        gk_o[...] = jnp.zeros(gk_o.shape, F32)

    @pl.when(k == 0)
    def _():
        ds[...] = ds_end[0].astype(F32)
        later[:, CHUNK : CHUNK + 8, :] = jnp.zeros((3, 8, later.shape[2]), F32)

    seg = segc[...]
    cums, cumst = cum[...], cumt[...]
    step = dt[...]
    xb, bb, cb, dyb = x[...], b[...], c[...], dy[...]
    xf, dyf = xb.astype(F32), dyb.astype(F32)
    row = lax.broadcasted_iota(jnp.int32, (CHUNK, CHUNK), 0)
    col = lax.broadcasted_iota(jnp.int32, (CHUNK, CHUNK), 1)
    linked = jnp.logical_and(col >= row, seg[:, 0:1] == segr[0:1, :])
    scores = mm_nt(bb, cb)
    d_scores = jnp.zeros((CHUNK, CHUNK), F32)
    direct, later_rows, d_inner = [], [], []
    for p in range(pairs):
        xp = xf[:, 128 * p : 128 * p + 128]
        dp = dyf[:, 128 * p : 128 * p + 128]
        xs = jnp.concatenate(
            [jnp.where(low, xp, 0.0).astype(BF16), jnp.where(low, 0.0, xp).astype(BF16)], axis=0
        )
        d_both = mm_nt(xs, dyb[:, 128 * p : 128 * p + 128])
        both = []
        for i in (0, 1):
            h = 2 * p + i
            fall = jnp.exp(jnp.where(linked, cumst[h : h + 1, :] - cums[:, h : h + 1], LOW))
            mixing = fall * scores
            d_mix = d_both[CHUNK * i : CHUNK * i + CHUNK, :]
            parts = mixing * d_mix
            scaled = d_mix * step[:, h : h + 1]
            d_scores = d_scores + fall * scaled
            direct.append(jnp.sum(parts, axis=1, keepdims=True))
            later_rows.append(jnp.sum(mixing * scaled, axis=0, keepdims=True))
            both.append(mixing.astype(BF16))
        dys = jnp.concatenate(
            [jnp.where(low, dp, 0.0).astype(BF16), jnp.where(low, 0.0, dp).astype(BF16)], axis=0
        )
        d_inner.append(mm(jnp.concatenate(both, axis=1), dys))
    pad = 8 - 2 * pairs
    direct = jnp.concatenate(direct + [jnp.zeros((CHUNK, pad), F32)], axis=1)
    later_rows = jnp.concatenate(later_rows + [jnp.zeros((pad, CHUNK), F32)], axis=0)
    d_inner = jnp.concatenate(d_inner, axis=1)

    state = sl[0, 0:states, :] + sl[0, states : states + 1, :] * s_in[0].astype(F32)
    d_state = ds[...]
    state_b, d_state_b = state.astype(BF16), d_state.astype(BF16)
    last = cums[CHUNK - 1 : CHUNK, :]
    to_end = jnp.where(seg[:, 5:6] > 0.5, jnp.exp(last - cums), 0.0)
    carried = jnp.where(seg[:, 4:5] > 0.5, jnp.exp(cums), 0.0)
    keep = expand(carried[CHUNK - 1 : CHUNK, :], pairs)
    to_end_x = expand(to_end, pairs)
    from_later = mm(bb, d_state_b) * to_end_x
    d_yc = dyf * expand(carried, pairs)
    d_ycb = d_yc.astype(BF16)
    q_dir = headsum(xf * from_later)
    r_in = headsum(d_yc * mm(cb, state_b))
    step_x = expand(step, pairs)
    d_x = step_x * (d_inner + from_later) + chan[1:2, :] * dyf
    xw = (xf * to_end_x * step_x).astype(BF16)
    d_sb = d_scores.astype(BF16)
    d_b = mm(d_sb, cb) + mm_nt(xw, d_state_b)
    d_c = mm_tn(d_sb, bb) + mm_nt(d_ycb, state_b)
    across = jnp.sum(d_state * state, axis=0, keepdims=True) * keep
    across = headsum(jnp.broadcast_to(across, (8, inner)))[0:1, :]
    ds[...] = keep * d_state + mm_tn(cb, d_ycb)
    q_in = q_dir * step
    d_a = sum_cols(upper_ones(), r_in - q_in - step * direct)
    d_a = d_a + (jnp.sum(q_in, axis=0, keepdims=True) + across)
    dac_o[:, 0:8] = d_a
    dac_o[:, 8:16] = q_dir + direct
    dat_o[...] = sum_rows(later_rows, lower_ones())

    cur = u[...].astype(F32)
    first = k == count - 1
    before = jnp.where(first, uhalo[...].astype(F32), uprev[...].astype(F32))
    ext[0:8, :] = before[8:16, :]
    ext[8 : 8 + CHUNK, :] = cur
    taps = kern[...]
    total = conv_total(ext, taps, seg, cur)
    sig = sigmoid(total)
    d_total = jnp.concatenate([d_x, d_b, d_c], axis=1) * (sig * (1.0 + total * (1.0 - sig)))
    gk_o[3:4, :] += jnp.sum(d_total * cur, axis=0, keepdims=True)
    gk_o[4:5, :] += jnp.sum(d_total, axis=0, keepdims=True)
    d_u = taps[3:4, :] * d_total
    halo = jnp.zeros((8, later.shape[2]), F32)
    for lagged in (1, 2, 3):
        lag = seg[:, lagged : lagged + 1] * d_total
        tap = taps[3 - lagged : 4 - lagged, :]
        gk_o[3 - lagged : 4 - lagged, :] += jnp.sum(
            lag * ext[pl.ds(8 - lagged, CHUNK), :], axis=0, keepdims=True
        )
        later[lagged - 1, 0:CHUNK, :] = lag
        d_u = d_u + tap * later[lagged - 1, pl.ds(lagged, CHUNK), :]
        later[lagged - 1, CHUNK : CHUNK + 8, :] = lag[0:8, :]
        edge[0:8, :] = jnp.zeros((8, later.shape[2]), F32)
        edge[8:16, :] = lag[0:8, :]
        halo = halo + tap * edge[pl.ds(lagged, 8), :]
    du_o[...] = d_u.astype(BF16)
    duh_o[0] = halo


class Plan:
    def __init__(self, block, inner, states, pos):
        self.block, self.inner, self.states, self.pos = block, inner, states, pos
        self.per_block = block // CHUNK
        self.half = self.per_block // 2
        self.count = 2 * self.per_block
        self.wide = inner + 2 * states

    def phys(self, s, k, pos):
        rel = s * 2 + ((k // self.per_block) ^ pos[0])
        half = ((k % self.per_block) // self.half) ^ pos[1]
        return half * (4 * self.half) + rel * self.half + k % self.half

    def seq(self, s, k, pos):
        return s * self.count + k

    def whole(self, s, k, pos):
        return (s ^ pos[2]) * self.count + k

    def call(self, kernel, ins, outs, scratch, args, backward=False, cost=None, name=None):
        last = self.count - 1

        def spec(kind, shape):
            def turn(k):
                return last - k if backward else k

            if kind == "phys":
                return pl.BlockSpec(shape, lambda s, k, pos: (self.phys(s, turn(k), pos), 0))
            if kind == "physT":
                return pl.BlockSpec(shape, lambda s, k, pos: (0, self.phys(s, turn(k), pos)))
            if kind == "seq":
                return pl.BlockSpec(shape, lambda s, k, pos: (self.seq(s, turn(k), pos), 0))
            if kind == "seqT":
                return pl.BlockSpec(shape, lambda s, k, pos: (0, self.seq(s, turn(k), pos)))
            if kind == "seq3":
                return pl.BlockSpec(shape, lambda s, k, pos: (self.seq(s, turn(k), pos), 0, 0))
            if kind == "whole":
                return pl.BlockSpec(shape, lambda s, k, pos: (self.whole(s, turn(k), pos), 0))
            if kind == "wholeT":
                return pl.BlockSpec(shape, lambda s, k, pos: (0, self.whole(s, turn(k), pos)))
            if kind == "prev":
                per = CHUNK // 16

                def before(s, k, pos):
                    k = turn(k)
                    return (self.phys(s, jnp.maximum(k - 1, 0), pos) * per + per - 1, 0)

                return pl.BlockSpec(shape, before)
            if kind == "stream":
                return pl.BlockSpec(shape, lambda s, k, pos: (s, 0))
            if kind == "stream3":
                return pl.BlockSpec(shape, lambda s, k, pos: (s, 0, 0))
            return pl.BlockSpec(shape, lambda s, k, pos: (0,) * len(shape))

        in_specs = [spec(*i) for i in ins]
        out_specs = [spec(kind, shape) for kind, shape, _, _ in outs]
        out_shape = [jax.ShapeDtypeStruct(full, dtype) for _, _, full, dtype in outs]
        return pl.pallas_call(
            kernel,
            grid_spec=pltpu.PrefetchScalarGridSpec(
                num_scalar_prefetch=1,
                grid=(2, self.count),
                in_specs=in_specs,
                out_specs=out_specs,
                scratch_shapes=scratch,
            ),
            out_shape=out_shape,
            compiler_params=pltpu.CompilerParams(dimension_semantics=("arbitrary", "arbitrary")),
            cost_estimate=cost,
            name=name,
        )(self.pos, *args)


class Grid:
    def __init__(self):
        self.nw, self.nc = lax.axis_size("weight"), lax.axis_size("context")
        w, c = lax.axis_index("weight"), lax.axis_index("context")
        self.wl, self.wh, self.cl, self.ch = w % 2, w // 2, c % 2, c // 2
        self.t = lax.axis_index("tensor")
        self.now, self.noc = self.nw // 2, self.nc // 2

    def hop(self, value, route):
        pairs = []
        for w in range(self.nw):
            for c in range(self.nc):
                to = route(w, c)
                if 0 <= to[0] < self.nw and 0 <= to[1] < self.nc:
                    pairs.append((w * self.nc + c, to[0] * self.nc + to[1]))
        return lax.ppermute(value, ("weight", "context"), pairs)

    def flip_x(self, value):
        return self.hop(value, lambda w, c: (w ^ 1, c))

    def flip_z(self, value):
        return self.hop(value, lambda w, c: (w, c ^ 1))

    def flip_xz(self, value):
        return self.hop(value, lambda w, c: (w ^ 1, c ^ 1))

    def turn_w(self, value, k):
        return self.hop(value, lambda w, c: ((w + 2 * k) % self.nw, c))

    def turn_c(self, value, k):
        return self.hop(value, lambda w, c: (w, (c + 2 * k) % self.nc))

    def swap(self, value):
        return lax.ppermute(value, "tensor", [(0, 1), (1, 0)])


def ordered(parts, me):
    n = len(parts)
    if n == 1:
        return parts[0][None]
    if n == 2:
        first, second = parts
        return jnp.stack([jnp.where(me == 0, first, second), jnp.where(me == 0, second, first)])
    return jnp.take(jnp.stack(parts), (me - jnp.arange(n)) % n, axis=0)


def by_group(parts, grid):
    both = [ordered(parts[0:2], grid.cl), ordered(parts[2:4], grid.cl)]
    return ordered(both, grid.wl)


def exchange(piece, grid):
    g = grid.wl * 2 + grid.cl
    return by_group(
        [
            piece(g),
            grid.flip_z(piece(g ^ 1)),
            grid.flip_x(piece(g ^ 2)),
            grid.flip_xz(piece(g ^ 3)),
        ],
        grid,
    )


def gather_owners(value, grid):
    over = [value] + [grid.turn_c(value, k) for k in range(1, grid.noc)]
    over = ordered(over, grid.ch)
    out = [over] + [grid.turn_w(over, k) for k in range(1, grid.now)]
    out = ordered(out, grid.wh)
    return jnp.transpose(out, (0, 2, 1, 3, 4, 5))


def pick(value, index, axis):
    return lax.dynamic_index_in_dim(value, index, axis, keepdims=False)


def reduce_owners(value, grid):
    total = pick(value, grid.wh, 0).astype(F32)
    for k in range(1, grid.now):
        sent = pick(value, (grid.wh + k) % grid.now, 0).astype(BF16)
        total = total + grid.turn_w(sent, k).astype(F32)
    value = total
    total = pick(value, grid.ch, 1)
    for k in range(1, grid.noc):
        sent = pick(value, (grid.ch + k) % grid.noc, 1).astype(BF16)
        total = total + grid.turn_c(sent, k).astype(F32)
    return total.astype(BF16)


def gather_tokens(rows, grid):
    half = rows.shape[0] // 2
    from_x, from_z = grid.flip_x(rows), grid.flip_z(rows)
    diag = [grid.flip_z(from_x[:half]), grid.flip_x(from_z[half:])]
    mine = jnp.concatenate([rows, from_z, from_x] + diag, axis=0)
    return jnp.concatenate([mine, grid.swap(mine)], axis=0)


def reduce_tokens(part, grid):
    rows = part.shape[0] // 2
    mine = part[:rows].astype(F32) + grid.swap(part[rows:].astype(BF16)).astype(F32)
    quarter = rows // 4
    half = quarter // 2
    own, at_z, at_x, diag = [mine[quarter * i : quarter * i + quarter] for i in range(4)]
    diag = diag.astype(BF16)
    for_z = grid.flip_x(diag[:half]).astype(F32)
    for_x = grid.flip_z(diag[half:]).astype(F32)
    at_z = jnp.concatenate([at_z[:half] + for_z, at_z[half:]], axis=0).astype(BF16)
    at_x = jnp.concatenate([at_x[:half], at_x[half:] + for_x], axis=0).astype(BF16)
    return own + grid.flip_x(at_x).astype(F32) + grid.flip_z(at_z).astype(F32)


def chain(state, through, grid, step):
    width = grid.nc

    def send(value):
        return grid.hop(value.astype(BF16), lambda w, c: (w, c + 2 * step))

    entering = send(state)
    for _ in range(grid.noc - 2):
        entering = send(state + through * entering.astype(F32))
    return entering


def sum_group(value, grid):
    value = value + grid.swap(value)
    return value + grid.flip_x(value) + grid.flip_z(value) + grid.flip_xz(value)


def sum_outer(value, grid):
    total = value
    for k in range(1, grid.noc):
        total = total + grid.turn_c(value, k)
    out = total
    for k in range(1, grid.now):
        out = out + grid.turn_w(total, k)
    return out


def both_halves(half, grid):
    other = grid.swap(half)
    first = jnp.where(grid.t == 0, half, other)
    second = jnp.where(grid.t == 0, other, half)
    return jnp.concatenate([first, second], axis=0)


def dot(a, b, dims, dtype=F32):
    return lax.dot_general(a, b, (dims, ((), ())), preferred_element_type=F32).astype(dtype)


def per_device(
    hidden, segment_ids, out_grad, in_gain, proj_gate, proj_input, proj_bc, proj_step,
    conv_input, conv_bc, conv_bias_in, conv_bias_bc, step_bias, decay_log, skip_gain,
    out_gain, proj_out,
):
    grid = Grid()
    length, model = hidden.shape
    heads_t = step_bias.shape[0]
    inner_t = conv_bias_in.shape[0]
    states = conv_bias_bc.shape[0] // 2
    total_inner = inner_t * lax.axis_size("tensor")
    rows = proj_gate.shape[0]
    heads, inner = heads_t // 4, inner_t // 4
    hd = inner // heads
    half = length // 2
    tokens = 4 * length
    g = grid.wl * 2 + grid.cl
    pos = jnp.stack([grid.cl, grid.t, grid.wl]).astype(jnp.int32)
    plan = Plan(length, inner, states, pos)
    n, blk = plan.count, CHUNK
    wide, seqs = plan.wide, 2 * n

    def columns(value, group, width, axis=1):
        return lax.dynamic_slice_in_dim(value, group * width, width, axis)

    bc_half = columns(proj_bc, grid.t, states)
    step_rows = jnp.pad(proj_step.T.reshape(4, heads, rows), ((0, 0), (0, 8 - heads), (0, inner + states - rows)))

    def first_piece(group):
        top = jnp.concatenate([columns(proj_input, group, inner), bc_half], axis=1)
        return jnp.concatenate([top, pick(step_rows, group, 0)], axis=0)

    first_w = gather_owners(exchange(first_piece, grid), grid)
    hid_f = hidden.astype(F32)
    inv_rms = lax.rsqrt(jnp.mean(hid_f * hid_f, axis=1, keepdims=True) + EPSILON)
    normed = (hid_f * inv_rms * in_gain[None, :]).astype(BF16)
    normed_all = gather_tokens(columns(normed, grid.t, half, 0), grid)

    edge_ids = jnp.pad(segment_ids[length - 3 :].astype(BF16)[None, :], ((0, 12), (0, model - 3)))
    edge = jnp.concatenate([edge_ids, normed[length - 3 :]], axis=0)
    edges = []
    for flip in (0, 1):
        near = grid.hop(edge, lambda w, c: (w ^ flip, c + 1 if c % 2 else -1))
        far = grid.hop(edge, lambda w, c: (w ^ flip, c + 2 if c % 2 else -1))
        edges.append(jnp.where(grid.cl == 0, near, far))
    edges = jnp.concatenate(edges, axis=0)

    seg_x, seg_z, seg_d = grid.flip_x(segment_ids), grid.flip_z(segment_ids), grid.flip_xz(segment_ids)
    streams = jnp.stack(
        [
            jnp.where(grid.cl == 0, jnp.concatenate([segment_ids, seg_z]), jnp.concatenate([seg_z, segment_ids])),
            jnp.where(grid.cl == 0, jnp.concatenate([seg_x, seg_d]), jnp.concatenate([seg_d, seg_x])),
        ]
    )
    edge_seg = edges.reshape(2, 16, model)[:, 0, 0:3].astype(jnp.int32)
    edge_seg = jnp.where(grid.ch == 0, -1, edge_seg)
    seg_ext = jnp.concatenate([edge_seg, streams], axis=1)
    span = 2 * length
    same = [seg_ext[:, 3 - j : 3 - j + span] == streams for j in (1, 2, 3)]
    by_chunk = streams.reshape(2, n, blk)
    chunk_prev = seg_ext[:, 2 : 2 + span].reshape(2, n, blk)[:, :, :1]
    link_prev = (by_chunk == chunk_prev).reshape(2, span)
    link_last = (by_chunk == by_chunk[:, :, blk - 1 :]).reshape(2, span)
    feats = jnp.stack(
        [v.astype(F32).reshape(2 * span) for v in [streams] + same + [link_prev, link_last]]
    )
    segr = jnp.pad(feats, ((0, 2), (0, 0)))
    segc = segr.T

    out_t = proj_out.T

    def gate_piece(group):
        return columns(proj_gate, group, inner)

    def out_piece(group):
        return columns(out_t, group, inner)

    gate_w = gather_owners(exchange(gate_piece, grid), grid).reshape(model, inner)
    out_w = gather_owners(exchange(out_piece, grid), grid).reshape(model, inner)
    cot_all = gather_tokens(columns(out_grad, grid.t, half, 0), grid)

    owners = first_w.reshape(model // rows, rows + 8, inner + states)
    input_w = owners[:, :rows, :inner].reshape(model, inner)
    bc_mine = owners[:, :rows, inner:].reshape(model, states)
    bc_other = grid.swap(bc_mine)
    bc_w = jnp.concatenate(
        [jnp.where(grid.t == 0, bc_mine, bc_other), jnp.where(grid.t == 0, bc_other, bc_mine)], axis=1
    )
    step_t = jnp.transpose(owners[:, rows:, :rows], (1, 0, 2)).reshape(8, model)
    first_cat = jnp.concatenate([input_w, bc_w], axis=1)
    u = dot(normed_all, first_cat, ((1,), (0,)), BF16)
    u_halo = dot(edges, first_cat, ((1,), (0,)), BF16)

    def heads_mine(v):
        return jnp.pad(lax.dynamic_slice_in_dim(v, g * heads, heads), (0, 8 - heads))

    bias, a_rate = heads_mine(step_bias), -jnp.exp(heads_mine(decay_log))
    a_rate = jnp.where(jnp.arange(8) < heads, a_rate, 0.0)
    skip_x = jnp.repeat(lax.dynamic_slice_in_dim(skip_gain, g * heads, heads), hd)
    gain = lax.dynamic_slice_in_dim(out_gain, g * inner, inner)
    hrow = jnp.pad(a_rate[None, :], ((0, 7), (0, 0)))
    hcol = hrow.T
    chan = jnp.pad(jnp.stack([gain, skip_x]), ((0, 6), (0, 0)))
    taps = jnp.concatenate(
        [
            jnp.concatenate([columns(conv_input, g, inner), conv_bc], axis=1),
            jnp.concatenate([lax.dynamic_slice_in_dim(conv_bias_in, g * inner, inner), conv_bias_bc])[None],
            jnp.zeros((3, wide), F32),
        ],
        axis=0,
    )
    raw = dot(normed_all, step_t, ((1,), (1,))) + bias[None, :]
    raw_t = dot(step_t, normed_all, ((1,), (1,))) + bias[:, None]
    dt, dt_t = jax.nn.softplus(raw), jax.nn.softplus(raw_t)

    def shape(*dims):
        return dims

    x, b_rows, c_rows, cum, cum_t, local, ends = plan.call(
        functools.partial(state_kernel, inner, states),
        [
            ("phys", (blk, wide)), ("prev", (16, wide)), ("stream", (16, wide)),
            ("phys", (blk, 8)), ("physT", (8, blk)), ("seq", (blk, 8)),
            ("all", (8, wide)), ("all", (8, 8)), ("all", (8, 8)),
        ],
        [
            ("seq", (blk, inner), (tokens, inner), BF16),
            ("seq", (blk, states), (tokens, states), BF16),
            ("seq", (blk, states), (tokens, states), BF16),
            ("seq", (blk, 8), (tokens, 8), F32),
            ("seqT", (8, blk), (8, tokens), F32),
            ("seq3", (1, states + 8, inner), (seqs, states + 8, inner), F32),
            ("stream3", (1, states + 8, inner), (2, states + 8, inner), F32),
        ],
        [pltpu.VMEM((blk + 8, wide), F32), pltpu.VMEM((states + 8, inner), F32)],
        (u, u, u_halo, dt, dt_t, segc, taps, hrow, hcol),
        name="block_states",
    )
    end_state, through = ends[:, :states], ends[:, states : states + 1]
    state_in = chain(end_state, through, grid, 1)
    (y_inner,) = plan.call(
        functools.partial(inner_kernel, inner, states),
        [
            ("seq", (blk, inner)), ("seq", (blk, states)), ("seq", (blk, states)), ("physT", (8, blk)),
            ("seq", (blk, 8)), ("seqT", (8, blk)), ("seq", (blk, 8)), ("seqT", (8, blk)),
        ],
        [("seq", (blk, inner), (tokens, inner), F32)],
        [],
        (x, b_rows, c_rows, dt_t, segc, segr, cum, cum_t),
        name="within_chunks",
    )
    gate_pre = dot(normed_all, gate_w, ((1,), (0,)), BF16)
    d_ynorm = dot(cot_all, out_w, ((1,), (0,)), BF16)
    y, gained, sums = plan.call(
        functools.partial(gate_kernel, inner, states),
        [
            ("seq", (blk, inner)), ("seq", (blk, inner)), ("seq", (blk, states)), ("seq", (blk, 8)),
            ("seq", (blk, 8)), ("seq3", (1, states + 8, inner)), ("stream3", (1, states, inner)),
            ("phys", (blk, inner)), ("phys", (blk, inner)), ("all", (8, inner)),
        ],
        [
            ("seq", (blk, inner), (tokens, inner), F32),
            ("phys", (blk, inner), (tokens, inner), BF16),
            ("wholeT", (2, blk), (2, tokens), F32),
        ],
        [],
        (y_inner, x, c_rows, cum, segc, local, state_in, gate_pre, d_ynorm, chan),
        name="gated_rows",
    )
    sums = sum_group(sums, grid)
    inv_out = lax.rsqrt(sums[0] / total_inner + EPSILON)
    coef = inv_out**3 * (sums[1] / total_inner)
    scal = jnp.pad(jnp.stack([inv_out, coef]), ((0, 6), (0, 0))).T

    mixed = reduce_tokens(dot(gained, out_w, ((1,), (1,))), grid)
    mine = (g * 2 + grid.t) * half
    inv_mine = lax.dynamic_slice_in_dim(inv_out, mine, half)[:, None]
    hid_half = columns(hid_f, grid.t, half, 0)
    result = both_halves((hid_half + mixed * inv_mine).astype(BF16), grid)

    d_y, d_gate, y_norm, acc, pulls = plan.call(
        functools.partial(pull_kernel, inner, states),
        [
            ("seq", (blk, inner)), ("seq", (blk, inner)), ("seq", (blk, states)), ("seq", (blk, 8)),
            ("seq", (blk, 8)), ("seq3", (1, states + 8, inner)),
            ("phys", (blk, inner)), ("phys", (blk, inner)), ("whole", (blk, 8)), ("all", (8, inner)),
        ],
        [
            ("seq", (blk, inner), (tokens, inner), BF16),
            ("phys", (blk, inner), (tokens, inner), BF16),
            ("phys", (blk, inner), (tokens, inner), BF16),
            ("all", (8, inner), (8, inner), F32),
            ("stream3", (1, states, inner), (2, states, inner), F32),
        ],
        [],
        (y, x, c_rows, cum, segc, local, gate_pre, d_ynorm, scal, chan),
        name="gated_back",
    )
    state_end = chain(pulls, through, grid, -1)

    g_out = dot(cot_all, y_norm, ((0,), (0,)))
    g_gate = dot(normed_all, d_gate, ((0,), (0,)))

    def to_owners(value):
        return reduce_owners(value.reshape(grid.now, 2, grid.noc, 2, -1, value.shape[-1]), grid)

    def from_groups(value):
        parts = exchange(lambda group: pick(value.reshape(4, rows, inner), group, 0), grid)
        return jnp.transpose(parts.reshape(4, rows, inner), (1, 0, 2)).reshape(rows, inner_t)

    g_out_mine = from_groups(to_owners(g_out)).T.astype(F32)
    g_gate_mine = from_groups(to_owners(g_gate)).astype(F32)

    d_u, d_halo, d_ac, d_at, g_taps = plan.call(
        functools.partial(back_kernel, inner, states),
        [
            ("phys", (blk, wide)), ("prev", (16, wide)), ("stream", (16, wide)),
            ("phys", (blk, 8)), ("seq", (blk, 8)), ("seqT", (8, blk)), ("seq", (blk, 8)), ("seqT", (8, blk)),
            ("seq", (blk, inner)), ("seq", (blk, states)), ("seq", (blk, states)), ("seq", (blk, inner)),
            ("seq3", (1, states + 8, inner)), ("stream3", (1, states, inner)), ("stream3", (1, states, inner)),
            ("all", (8, wide)), ("all", (8, 8)), ("all", (8, inner)),
        ],
        [
            ("phys", (blk, wide), (tokens, wide), BF16),
            ("stream3", (1, 8, wide), (2, 8, wide), F32),
            ("phys", (blk, 16), (tokens, 16), F32),
            ("physT", (8, blk), (8, tokens), F32),
            ("all", (8, wide), (8, wide), F32),
        ],
        [
            pltpu.VMEM((blk + 8, wide), F32), pltpu.VMEM((3, blk + 8, wide), F32),
            pltpu.VMEM((16, wide), F32), pltpu.VMEM((states, inner), F32),
        ],
        (
            u, u, u_halo, dt, segc, segr, cum, cum_t, x, b_rows, c_rows, d_y, local, state_in, state_end,
            taps, hrow, chan,
        ),
        backward=True,
        name="block_back",
    )
    d_edge = grid.hop(d_halo.astype(BF16), lambda w, c: (w, c - 2))
    for s in (0, 1):
        row = plan.phys(s, n - 1, pos) * blk + blk - 8
        old = lax.dynamic_slice(d_u, (row, 0), (8, wide))
        d_u = lax.dynamic_update_slice(d_u, old + d_edge[s], (row, 0))
    d_a = d_ac[:, :8] + d_at.T
    d_dt = d_ac[:, 8:] + d_a * a_rate[None, :]
    g_decay = jnp.sum(d_a * dt, axis=0) * a_rate
    d_raw = d_dt * jax.nn.sigmoid(raw)
    g_bias = jnp.sum(d_raw, axis=0)
    d_step = d_raw.astype(BF16)

    g_first = dot(normed_all, d_u, ((0,), (0,)))
    g_step_t = dot(d_step, normed_all, ((0,), (0,)))
    d_normed = (
        dot(d_u, first_cat, ((1,), (1,)))
        + dot(d_gate, gate_w, ((1,), (1,)))
        + dot(d_step, step_t, ((1,), (0,)))
    )
    g_gain = (
        jnp.sum(first_cat.astype(F32) * g_first, axis=1)
        + jnp.sum(gate_w.astype(F32) * g_gate, axis=1)
        + jnp.sum(step_t.astype(F32) * g_step_t, axis=0)
    ) / in_gain

    bc_parts = g_first[:, inner:]
    bc_sum = columns(bc_parts, grid.t, states) + grid.swap(
        columns(bc_parts, 1 - grid.t, states).astype(BF16)
    ).astype(F32)
    step_part = jnp.transpose(g_step_t.reshape(8, model // rows, rows), (1, 0, 2))
    step_part = jnp.pad(step_part, ((0, 0), (0, 0), (0, inner + states - rows)))
    first_part = jnp.concatenate([g_first[:, :inner], bc_sum], axis=1).reshape(model // rows, rows, -1)
    first_part = jnp.concatenate([first_part, step_part], axis=1)
    first_sum = to_owners(first_part.reshape(model // rows * (rows + 8), -1)).reshape(4, rows + 8, -1)
    got = exchange(lambda group: pick(first_sum, group, 0), grid).reshape(4, rows + 8, -1)
    g_input_mine = jnp.transpose(got[:, :rows, :inner], (1, 0, 2)).reshape(rows, inner_t).astype(F32)
    g_bc_mine = jnp.sum(got[:, :rows, inner:].astype(F32), axis=0)
    g_bc_other = grid.swap(g_bc_mine)
    g_bc_full = jnp.concatenate(
        [jnp.where(grid.t == 0, g_bc_mine, g_bc_other), jnp.where(grid.t == 0, g_bc_other, g_bc_mine)], axis=1
    )
    g_step_mine = got[:, rows : rows + heads, :rows].reshape(heads_t, rows).T.astype(F32)

    def spread(v):
        return lax.dynamic_update_slice(jnp.zeros((v.shape[0], inner_t), F32), v, (0, g * inner))

    g_skip = jnp.sum(acc[1].reshape(heads, hd), axis=1)
    per_head = jnp.stack([g_decay[:heads], g_skip, g_bias[:heads]])
    per_head = lax.dynamic_update_slice(jnp.zeros((3, heads_t), F32), per_head, (0, g * heads))
    per_head = jnp.pad(per_head, ((0, 0), (0, inner_t - heads_t)))
    own = jnp.concatenate([spread(g_taps[:5, :inner]), spread(acc[:1]), per_head], axis=0)
    shared = jnp.concatenate([g_gain, g_taps[:5, inner:].reshape(-1)])
    shared = shared + grid.swap(shared)
    flat = jnp.concatenate([own.reshape(-1), shared])
    flat = jnp.pad(flat, (0, -flat.shape[0] % 1024)).reshape(-1, 128)
    flat = sum_outer(flat, grid)
    flat = flat + grid.flip_x(flat)
    flat = (flat + grid.flip_z(flat)).reshape(-1)
    own = flat[: 9 * inner_t].reshape(9, inner_t)
    s_gain = flat[9 * inner_t : 9 * inner_t + model]
    s_bc = flat[9 * inner_t + model : 9 * inner_t + model + 10 * states].reshape(5, 2 * states)

    d_half = reduce_tokens(d_normed, grid)
    inv_half = columns(inv_rms, grid.t, half, 0)
    d_scaled = d_half * in_gain[None, :]
    d_hid = (
        inv_half * d_scaled
        - hid_half * inv_half**3 * jnp.mean(hid_half * d_scaled, axis=1, keepdims=True)
        + columns(out_grad, grid.t, half, 0).astype(F32)
    )
    d_hidden = both_halves(d_hid, grid)
    return (
        result, d_hidden, s_gain, g_gate_mine, g_input_mine, g_bc_full, g_step_mine,
        own[:4], s_bc[:4], own[4], s_bc[4], own[8, :heads_t], own[6, :heads_t], own[7, :heads_t],
        own[5], g_out_mine,
    )


def solution(mesh):
    rows = P(("weight", "context"), None)
    both = P(("weight", "context"), "tensor")
    chan = P("tensor")
    out_cols = P("tensor", ("weight", "context"))
    return jax.shard_map(
        per_device,
        mesh=mesh,
        in_specs=(
            rows, P(("weight", "context")), rows, P(), both, both, rows, both,
            P(None, "tensor"), P(), chan, P(), chan, chan, chan, chan, out_cols,
        ),
        out_specs=(
            rows, rows, P(), both, both, rows, both,
            P(None, "tensor"), P(), chan, P(), chan, chan, chan, chan, out_cols,
        ),
        check_vma=False,
    )
```
